512 devices in a mesh: req: 8 (over x, core), vocab: 64 (over y, z).
Axes of the slice: x: 4, y: 4, z: 16, core: 2. Of those that a mesh axis runs over, the one named last changes fastest.
Arguments:
- hidden: bfloat16 [8192, 2304], P(('req', 'vocab'))
- norm_gain: float32 [2304], replicated, may hold values from 0.5 to 1.5
- head_weight: bfloat16 [2304, 65536], P(None, 'vocab')
- targets: int32 [8192], P(('req', 'vocab')), may hold values from 0 to 65535
- counts: int32 [512], P(('req', 'vocab')), may hold values from 5 to 10, as said below
Outputs:
- logprob: float32 [8192], P(('req', 'vocab'))
- entropy: float32 [8192], P(('req', 'vocab'))
The draws below stay inside these ranges and needn't reach their ends.
Inputs may be any that keep to these rules, and one draw needn't show every extreme that they name: The scored slots of a device are its first counts slots; some device holds exactly 10.
All inputs are finite; a program needn't handle non-finite values.
Results may differ from the reference program's by a relative error of at most 0.012.
The reference program's roundings to bfloat16 on the way (of `normed`) count: a program that leaves them out, or rounds other values in their place, can miss the bound.
Values may be sent and summed in bfloat16 or wider, within the bound.
A program may use at most 64 MiB of HBM per device.

```python
import math
import jax
import jax.numpy as jnp
from jax import lax

D = 2304
SLOTS = 16
CAP = 10
VOCAB = 65536
ROWS = 8192


def base_weight(key):
    return jax.random.normal(jax.random.fold_in(key, 11), (D, VOCAB), jnp.float32)


def draw_head_weight(key, part):
    values = base_weight(key)
    return (values * (5000.0 / D)).astype(jnp.bfloat16)


def draw_hidden(key, part):
    noise = jax.random.normal(jax.random.fold_in(key, 21), (ROWS, D), jnp.float32)
    row_scale = jnp.exp(jax.random.uniform(jax.random.fold_in(key, 22), (ROWS, 1), jnp.float32) * 2.302585)
    col_scale = jnp.exp(jax.random.uniform(jax.random.fold_in(key, 23), (1, D), jnp.float32) * 2.302585)
    values = noise * row_scale * col_scale
    weight = base_weight(key)
    first = jax.random.randint(jax.random.fold_in(key, 24), (ROWS,), 0, VOCAB)
    second = jax.random.randint(jax.random.fold_in(key, 25), (ROWS,), 0, VOCAB)
    picked = jax.random.randint(jax.random.fold_in(key, 26), (ROWS,), 0, 8) == 0
    power = jax.random.randint(jax.random.fold_in(key, 27), (ROWS,), -2, 3).astype(jnp.float32)
    strength = jnp.exp(power * 0.693147)
    aligned = strength[:, None] * (weight[:, first].T + 0.99 * weight[:, second].T) + noise
    values = jnp.where(picked[:, None], aligned, values)
    return values.astype(jnp.bfloat16)


def draw_counts(key, part):
    owners = ROWS // SLOTS
    drawn = jax.random.randint(jax.random.fold_in(key, 31), (owners,), CAP // 2, CAP + 1)
    fullest = jax.random.randint(jax.random.fold_in(key, 32), (), 0, owners)
    return drawn.at[fullest].set(CAP).astype(jnp.int32)


def plant(result, own_key, low, largest):
    dims = result.shape
    index_at = [jax.random.randint(jax.random.fold_in(own_key, axis), (), 0, dims[axis]) for axis in range(len(dims))]
    result = result.at[tuple(index_at)].set(low)
    longest = dims.index(max(dims))
    index_at[longest] = (index_at[longest] + 1) % dims[longest]
    return result.at[tuple(index_at)].set(largest)


def setup_inputs(seed: int = 0) -> dict:
    keys = jax.random.split(jax.random.key(seed), 6)
    return {
        "hidden": draw_hidden(jax.random.fold_in(keys[5], 71), 0),
        "norm_gain": jnp.clip(1.0 + 0.1 * jax.random.normal(keys[1], (D,), jnp.float32), 0.5, 1.5),
        "head_weight": draw_head_weight(jax.random.fold_in(keys[5], 71), 0),
        "targets": plant(jax.random.randint(keys[3], (ROWS,), 0, VOCAB), jax.random.fold_in(keys[3], 1), 0, VOCAB - 1).astype(jnp.int32),
        "counts": draw_counts(jax.random.fold_in(keys[5], 71), 0),
    }


logit_scale = 256.0 / 2304.0

def reference(hidden, norm_gain, head_weight, targets, counts):
    values = hidden.astype(jnp.float32)
    square_mean = lax.optimization_barrier(jnp.mean(values * values, axis=1, keepdims=True))
    normed = (values * lax.rsqrt(square_mean + 1e-05) * norm_gain[None, :]).astype(jnp.bfloat16)
    block = math.gcd(ROWS, 512)

    def block_stats(pair):
        rows_blk, target_blk = pair
        logits = jnp.dot(rows_blk, head_weight, preferred_element_type=jnp.float32) * logit_scale
        peak = lax.optimization_barrier(jnp.max(logits, axis=1))
        weights = jnp.exp(logits - peak[:, None])
        total = lax.optimization_barrier(jnp.sum(weights, axis=1))
        moment = lax.optimization_barrier(jnp.sum(weights * logits, axis=1))
        chosen = jnp.take_along_axis(logits, target_blk[:, None], axis=1)[:, 0]
        return (chosen - peak - jnp.log(total), peak + jnp.log(total) - moment / total)
    logp, entr = lax.map(block_stats, (normed.reshape(ROWS // block, block, D), targets.reshape(ROWS // block, block)))
    logp = logp.reshape(ROWS)
    entr = entr.reshape(ROWS)
    slot_index = jnp.arange(ROWS, dtype=jnp.int32)
    scored = slot_index % SLOTS < jnp.repeat(counts, SLOTS)
    logprob = jnp.where(scored, logp, jnp.float32(0.0))
    entropy = jnp.where(scored, entr, jnp.float32(0.0))
    return (logprob, entropy)
```

```python
import jax
import jax.numpy as jnp
from jax import lax
from jax.experimental import pallas as pl
from jax.experimental.pallas import tpu as pltpu
from jax.sharding import PartitionSpec as P

logit_scale = 256.0 / 2304.0
NY, NZ = 4, 16
CAP = 10
MAIN = 8
REST = CAP - MAIN
SPLIT = 1920
EXTRA = 128


def kernel(
    hidden_hbm, gain_hbm, weight_hbm, targets_ref, counts_ref,
    logprob_ref, entropy_ref,
    hid, gain, weight, za, yb, rl, rest32, block, logits, turn, stat_out, stat_in, sum_out, sum_in,
    local_sem, za_s, za_r, zb_s, zb_r, zr_s, zr_r, ya_s, ya_r, yh_s, yh_r,
    b0_s, b0_r, r0_s, r0_r, st_s, st_r, s2_s, s2_r,
):
    depth = hid.shape[1]
    half = (SPLIT // 256 + 1) // 1 * 128 if (SPLIT // 128) % 2 else SPLIT // 2
    vocab_dev = weight.shape[1]
    me = lax.axis_index("vocab")
    my_y, my_z = me // NZ, lax.rem(me, NZ)

    def at(y, z):
        return {"vocab": lax.rem(y + NY, NY) * NZ + lax.rem(z + NZ, NZ)}

    near = [at(my_y, my_z + 1), at(my_y, my_z - 1), at(my_y + 1, my_z), at(my_y - 1, my_z), at(my_y + 2, my_z)]
    barrier = pltpu.get_barrier_semaphore()
    for device in near:
        pl.semaphore_signal(barrier, inc=1, device_id=device, device_id_type=pl.DeviceIdType.MESH)
    fetch_hidden = pltpu.make_async_copy(hidden_hbm, hid, local_sem.at[0])
    fetch_gain = pltpu.make_async_copy(gain_hbm, gain, local_sem.at[1])
    fetch_weight = pltpu.make_async_copy(weight_hbm, weight, local_sem.at[2])
    fetch_hidden.start()
    fetch_gain.start()
    fetch_weight.start()

    def remote(src, dst, send, recv, device):
        return pltpu.make_async_remote_copy(
            src_ref=src, dst_ref=dst, send_sem=send, recv_sem=recv,
            device_id=device, device_id_type=pl.DeviceIdType.MESH,
        )

    def plane(way, hop):
        return hop if way == 0 else lax.rem(NZ - hop, NZ)

    def z_main(way, hop):
        src, dst = plane(way, hop - 1), plane(way, hop)
        return remote(za.at[src, 0], za.at[dst, 0], za_s.at[way, hop], za_r.at[way, hop], near[way])

    def z_main_half(way):
        last = NZ // 2
        cols = pl.ds(0, half) if way == 0 else pl.ds(half, SPLIT - half)
        src = plane(way, last - 1)
        return remote(
            za.at[src, 0, :, cols], za.at[last, 0, :, cols], za_s.at[way, last], za_r.at[way, last], near[way]
        )

    def z_side(way, hop):
        src, dst = plane(way, hop - 1), plane(way, hop)
        return [
            remote(rl.at[src], rl.at[dst], zr_s.at[way, hop], zr_r.at[way, hop], near[way]),
            remote(yb.at[src], yb.at[dst], zb_s.at[way, hop], zb_r.at[way, hop], near[way]),
        ]

    def z_side_half(way):
        last = NZ // 2
        src = plane(way, last - 1)
        part = pl.ds(0, NY // 2) if way == 0 else pl.ds(NY // 2, NY // 2)
        return [
            remote(rl.at[src, part], rl.at[last, part], zr_s.at[way, last], zr_r.at[way, last], near[way]),
            remote(yb.at[src, part], yb.at[last, part], zb_s.at[way, last], zb_r.at[way, last], near[way]),
        ]

    def y_main(p, way):
        slot = 1 if way == 0 else NY - 1
        return remote(za.at[p, 0], za.at[p, slot], ya_s.at[p, way], ya_r.at[p, way], near[2 + way])

    def y_half(p, way):
        slot = 1 if way == 0 else NY - 1
        cols = pl.ds(0, half) if way == 0 else pl.ds(half, SPLIT - half)
        return remote(
            za.at[p, slot, :, cols], za.at[p, 2, :, cols], yh_s.at[p, way], yh_r.at[p, way], near[2 + way]
        )

    y_near = {1: near[2], 2: near[4], 3: near[3]}

    def y_side(j):
        return [
            remote(rl.at[0, 0], rl.at[0, j], r0_s.at[j], r0_r.at[j], y_near[j]),
            remote(yb.at[0, 0], yb.at[0, j], b0_s.at[j], b0_r.at[j], y_near[j]),
        ]

    def stat_copy(p):
        device = at(my_y, my_z - p)
        return remote(stat_out.at[p], stat_in.at[p], st_s.at[p], st_r.at[p], device)

    def sum_copy(j):
        return remote(sum_out, sum_in.at[j], s2_s.at[j], s2_r.at[j], {1: near[3], 2: near[4], 3: near[2]}[j])

    def start(copies):
        for copy in copies:
            copy.start()

    def arrive(copies):
        for copy in copies:
            copy.wait_recv()

    fetch_hidden.wait()
    fetch_gain.wait()
    values = hid[...].astype(jnp.float32)
    square_mean = jnp.mean(values * values, axis=1, keepdims=True)
    normed = values * lax.rsqrt(square_mean + 1e-05) * gain[...]
    rows = normed.astype(jnp.bfloat16)
    za[0, 0] = rows[0:MAIN, 0:SPLIT]
    yb[0, 0] = rows[0:MAIN, SPLIT:depth]
    rl[0, 0, :, 0:depth] = normed[MAIN:CAP].astype(jnp.bfloat16)
    wanted = jnp.broadcast_to(targets_ref[...], (REST, EXTRA))
    first = lax.broadcasted_iota(jnp.int32, (REST, EXTRA), 0) == 0
    digits = jnp.where(first, wanted >> 8, wanted & 255)
    rl[0, 0, :, depth : depth + EXTRA] = digits.astype(jnp.float32).astype(jnp.bfloat16)
    turn[...] = jnp.zeros_like(turn)

    pl.semaphore_wait(barrier, len(near))
    for j in (1, 3, 2):
        start(y_side(j))
    for way in (0, 1):
        start([z_main(way, 1)])
    for way in (0, 1):
        start([y_main(0, way)])
    for j in (1, 3, 2):
        arrive(y_side(j))
    for way in (0, 1):
        start(z_side(way, 1))

    lane = lax.broadcasted_iota(jnp.int32, (8, 128), 1)
    sub = lax.broadcasted_iota(jnp.int32, (8, 128), 0)
    start_column = (me * vocab_dev).astype(jnp.float32)

    def fill(p, base):
        for j in range(NY):
            block[base + MAIN * j : base + MAIN * (j + 1), 0:SPLIT] = za[p, j].astype(jnp.float32)
            block[base + MAIN * j : base + MAIN * (j + 1), SPLIT:depth] = yb[p, j].astype(jnp.float32)
        for j in range(NY):
            rest32[REST * j : REST * (j + 1), :] = rl[p, j].astype(jnp.float32)
        block[base + MAIN * NY : base + CAP * NY, :] = rest32[:, 0:depth]
        digits8 = rest32[:, depth : depth + EXTRA]
        columns = []
        last = jnp.zeros((8, 128), jnp.float32)
        for j in range(NY):
            ids = digits8[2 * j : 2 * j + 1] * 256.0 + digits8[2 * j + 1 : 2 * j + 2]
            ids = jnp.broadcast_to(ids, (8, 128))
            columns.append(jnp.sum(jnp.where(lane == sub, ids, 0.0), axis=1, keepdims=True))
            last = jnp.where(sub // REST == j, ids, last)
        columns.append(jnp.sum(jnp.where(lane == MAIN + lax.rem(sub, REST), last, 0.0), axis=1, keepdims=True))
        return columns

    pair = 2 * CAP * NY

    def compute(q):
        low = q
        high = jnp.where(q == NZ // 2, 0, NZ - q)
        columns = fill(low, 0) + fill(high, CAP * NY)
        wanted_column = jnp.concatenate(columns, axis=0) - start_column
        lhs = block[...].astype(jnp.bfloat16)
        for n in range(0, vocab_dev, 256):
            logits[:, n : n + 256] = (
                jnp.dot(lhs, weight[:, n : n + 256], preferred_element_type=jnp.float32) * logit_scale
            )
        z = logits[...]
        peak = jnp.max(z, axis=1, keepdims=True)
        e = jnp.exp(z - peak)
        total = jnp.sum(e, axis=1, keepdims=True)
        moment = jnp.sum(e * z, axis=1, keepdims=True)
        column = lax.broadcasted_iota(jnp.int32, z.shape, 1).astype(jnp.float32)
        chosen = jnp.sum(jnp.where(column == wanted_column, z, 0.0), axis=1, keepdims=True)
        side = lax.broadcasted_iota(jnp.int32, (pair, 128), 1)
        turn[0:pair, :] = jnp.where(
            side == 0, peak, jnp.where(side == 1, total, jnp.where(side == 2, moment, chosen))
        )
        turned = jnp.transpose(turn[...])[0:8]
        stat_out[low] = turned
        stat_out[high] = pltpu.roll(turned, 128 - CAP * NY, 1)
        start([stat_copy(low)])

        @pl.when(q < NZ // 2)
        def _():
            start([stat_copy(high)])

    last_hop = NZ // 2

    def step(hop, carry):
        @pl.when(hop < last_hop)
        def _():
            for way in (0, 1):
                arrive([z_main(way, hop)])

            @pl.when(hop < last_hop - 1)
            def _():
                for way in (0, 1):
                    start([z_main(way, hop + 1)])

            @pl.when(hop == last_hop - 1)
            def _():
                for way in (0, 1):
                    start([z_main_half(way)])

            for p in (plane(0, hop), plane(1, hop)):
                for way in (0, 1):
                    start([y_main(p, way)])
            for way in (0, 1):
                arrive(z_side(way, hop))

            @pl.when(hop < last_hop - 1)
            def _():
                for way in (0, 1):
                    start(z_side(way, hop + 1))

            @pl.when(hop == last_hop - 1)
            def _():
                for way in (0, 1):
                    start(z_side_half(way))

        @pl.when(hop == last_hop)
        def _():
            for way in (0, 1):
                arrive([z_main_half(way)])
            for way in (0, 1):
                start([y_main(last_hop, way)])
            for way in (0, 1):
                arrive(z_side_half(way))

        @pl.when(hop <= last_hop + 1)
        def _():
            q = hop - 1

            def second(p):
                for way in (0, 1):
                    arrive([y_main(p, way)])
                    start([y_half(p, way)])

            second(q)

            @pl.when(jnp.logical_and(q > 0, q < last_hop))
            def _():
                second(NZ - q)

        @pl.when(hop == 3)
        def _():
            fetch_weight.wait()

        @pl.when(hop >= 3)
        def _():
            q = hop - 2
            for p in (q, jnp.where(q == last_hop, 0, NZ - q)):
                for way in (0, 1):
                    arrive([y_half(p, way)])
            compute(q)

        return carry

    lax.fori_loop(1, last_hop + 3, step, 0)

    def merge(peaks, totals, moments, chosens):
        peak = jnp.max(peaks, axis=0, keepdims=True)
        factor = jnp.exp(peaks - peak)
        return (
            peak,
            jnp.sum(totals * factor, axis=0, keepdims=True),
            jnp.sum(moments * factor, axis=0, keepdims=True),
            jnp.sum(chosens, axis=0, keepdims=True),
        )

    stat_in[0] = stat_out[0]

    def await_stat(p, carry):
        arrive([stat_copy(p)])
        return carry

    lax.fori_loop(1, NZ, await_stat, 0)
    peak, total, moment, chosen = merge(stat_in[:, 0], stat_in[:, 1], stat_in[:, 2], stat_in[:, 3])
    sums = jnp.where(sub == 0, peak, jnp.where(sub == 1, total, jnp.where(sub == 2, moment, chosen)))
    sum_out[...] = sums
    sum_in[0] = sums
    for j in (2, 1, 3):
        start([sum_copy(j)])
    for j in (1, 3, 2):
        arrive([sum_copy(j)])
    mine = []
    for j in range(NY):
        tile = sum_in[j]
        body = pltpu.roll(tile, (128 - MAIN * j) % 128, 1)
        tail = pltpu.roll(tile, (128 + MAIN - MAIN * NY - REST * j) % 128, 1)
        mine.append(jnp.where(lane < MAIN, body, tail))
    peak, total, moment, chosen = merge(
        *[jnp.concatenate([tile[i : i + 1] for tile in mine], axis=0) for i in range(4)]
    )
    log_total = jnp.log(total)
    scored = lax.broadcasted_iota(jnp.int32, (1, 128), 1) < counts_ref[0]
    slots = logprob_ref.shape[1]
    logprob_ref[...] = jnp.where(scored, chosen - peak - log_total, 0.0)[:, 0:slots]
    entropy_ref[...] = jnp.where(scored, peak + log_total - moment / total, 0.0)[:, 0:slots]

    for j in (1, 2, 3):
        for copy in y_side(j):
            copy.wait_send()
        sum_copy(j).wait_send()

    def sent_z(hop, carry):
        for way in (0, 1):
            z_main(way, hop).wait_send()
            for copy in z_side(way, hop):
                copy.wait_send()
        return carry

    lax.fori_loop(1, last_hop, sent_z, 0)
    for way in (0, 1):
        z_main_half(way).wait_send()
        for copy in z_side_half(way):
            copy.wait_send()

    def sent_y(p, carry):
        for way in (0, 1):
            y_main(p, way).wait_send()
            y_half(p, way).wait_send()
        return carry

    lax.fori_loop(0, NZ, sent_y, 0)

    def sent_stat(p, carry):
        stat_copy(p).wait_send()
        return carry

    lax.fori_loop(1, NZ, sent_stat, 0)


def on_device(hidden, norm_gain, head_weight, targets, counts):
    slots, depth = hidden.shape
    vocab_dev = head_weight.shape[1]
    dma = pltpu.SemaphoreType.DMA
    hops = NZ // 2 + 1
    any_spec = pl.BlockSpec(memory_space=pl.ANY)
    vmem_spec = pl.BlockSpec(memory_space=pltpu.VMEM)
    wanted = jnp.pad(targets[None, :], ((0, 0), (0, EXTRA - slots)))
    logprob, entropy = pl.pallas_call(
        kernel,
        out_shape=(
            jax.ShapeDtypeStruct((1, slots), jnp.float32),
            jax.ShapeDtypeStruct((1, slots), jnp.float32),
        ),
        in_specs=[any_spec, any_spec, any_spec, vmem_spec, pl.BlockSpec(memory_space=pltpu.SMEM)],
        out_specs=(vmem_spec, vmem_spec),
        scratch_shapes=[
            pltpu.VMEM((slots, depth), jnp.bfloat16),
            pltpu.VMEM((1, depth), jnp.float32),
            pltpu.VMEM((depth, vocab_dev), jnp.bfloat16),
            pltpu.VMEM((NZ, NY, MAIN, SPLIT), jnp.bfloat16),
            pltpu.VMEM((NZ, NY, MAIN, depth - SPLIT), jnp.bfloat16),
            pltpu.VMEM((NZ, NY, REST, depth + EXTRA), jnp.bfloat16),
            pltpu.VMEM((NY * REST, depth + EXTRA), jnp.float32),
            pltpu.VMEM((2 * NY * CAP, depth), jnp.float32),
            pltpu.VMEM((2 * NY * CAP, vocab_dev), jnp.float32),
            pltpu.VMEM((128, 128), jnp.float32),
            pltpu.VMEM((NZ, 8, 128), jnp.float32),
            pltpu.VMEM((NZ, 8, 128), jnp.float32),
            pltpu.VMEM((8, 128), jnp.float32),
            pltpu.VMEM((NY, 8, 128), jnp.float32),
            dma((3,)),
            dma((2, hops)), dma((2, hops)),
            dma((2, hops)), dma((2, hops)),
            dma((2, hops)), dma((2, hops)),
            dma((NZ, 2)), dma((NZ, 2)),
            dma((NZ, 2)), dma((NZ, 2)),
            dma((NY,)), dma((NY,)),
            dma((NY,)), dma((NY,)),
            dma((NZ,)), dma((NZ,)),
            dma((NY,)), dma((NY,)),
        ],
        compiler_params=pltpu.CompilerParams(collective_id=0, has_side_effects=True),
    )(hidden, norm_gain[None, :], head_weight, wanted, counts)
    return (logprob.reshape(slots), entropy.reshape(slots))


def solution(mesh):
    in_specs = (
        P(("req", "vocab"), None),
        P(),
        P(None, "vocab"),
        P(("req", "vocab")),
        P(("req", "vocab")),
    )
    out_specs = (P(("req", "vocab")), P(("req", "vocab")))
    return jax.shard_map(
        on_device, mesh=mesh, in_specs=in_specs, out_specs=out_specs, check_vma=False
    )
```

```python
import jax
import jax.numpy as jnp
from jax import lax
from jax.experimental import pallas as pl
from jax.experimental.pallas import tpu as pltpu
from jax.sharding import PartitionSpec as P

logit_scale = 256.0 / 2304.0
NY, NZ = 4, 16
CAP = 10
MAIN = 8
REST = CAP - MAIN
EXTRA = 128
ROWS = CAP * NY
LAST = NZ // 2
SOURCE = {4: 0, 1: 0, 2: 1, 6: 4, 5: 4, 3: 2, 7: 6, 8: 6}
BLOCKS = 4
WAYS = (1, -1)


def plane(way, k):
    return k * way % NZ


def kernel(
    hidden_hbm, gain_hbm, weight_hbm, targets_hbm, counts_hbm,
    out_ref,
    hid, gain, weight, ids, held, main, rest, rest32, block, logits, turn, stat_out, stat_in, sum_out, sum_in,
    local_sem, zm_s, zm_r, zr_s, zr_r, ym_s, ym_r, yh_s, yh_r, r0_s, r0_r, st_s, st_r, s2_s, s2_r,
):
    depth = hid.shape[1]
    half = depth // 2
    vocab_dev = weight.shape[1]
    me = lax.axis_index("vocab")
    my_y, my_z = me // NZ, lax.rem(me, NZ)

    def at(dy, dz):
        return {"vocab": lax.rem(my_y + dy + NY, NY) * NZ + lax.rem(my_z + dz + NZ, NZ)}

    reach = sorted({k - SOURCE[k] for k in SOURCE})
    near = [at(0, way * k) for k in reach for way in WAYS] + [at(dy, 0) for dy in range(1, NY)]
    barrier = pltpu.get_barrier_semaphore()
    for device in near:
        pl.semaphore_signal(barrier, inc=1, device_id=device, device_id_type=pl.DeviceIdType.MESH)
    fetches = [
        pltpu.make_async_copy(src, dst, local_sem.at[i])
        for i, (src, dst) in enumerate(
            [(hidden_hbm, hid), (gain_hbm, gain), (targets_hbm, ids), (counts_hbm, held), (weight_hbm, weight)]
        )
    ]
    for fetch in fetches:
        fetch.start()

    def remote(src, dst, send, recv, device):
        return pltpu.make_async_remote_copy(
            src_ref=src, dst_ref=dst, send_sem=send, recv_sem=recv,
            device_id=device, device_id_type=pl.DeviceIdType.MESH,
        )

    def z_main(way, k):
        src, dst = plane(way, SOURCE[k]), plane(way, k)
        device = at(0, way * (k - SOURCE[k]))
        if k < LAST:
            return remote(main.at[src, 0], main.at[dst, 0], zm_s.at[dst], zm_r.at[dst], device)
        cols = pl.ds(0, half) if way == 1 else pl.ds(half, half)
        sem = LAST if way == 1 else NZ
        return remote(main.at[src, 0, :, cols], main.at[dst, 0, :, cols], zm_s.at[sem], zm_r.at[sem], device)

    def z_rest(way, k):
        src, dst = plane(way, SOURCE[k]), plane(way, k)
        device = at(0, way * (k - SOURCE[k]))
        if k < LAST:
            return remote(rest.at[src], rest.at[dst], zr_s.at[dst], zr_r.at[dst], device)
        part = pl.ds(0, NY // 2) if way == 1 else pl.ds(NY // 2, NY // 2)
        sem = LAST if way == 1 else NZ
        return remote(rest.at[src, part], rest.at[dst, part], zr_s.at[sem], zr_r.at[sem], device)

    def y_main(p, way):
        slot = way % NY
        i = WAYS.index(way)
        return remote(main.at[p, 0], main.at[p, slot], ym_s.at[p, i], ym_r.at[p, i], at(way, 0))

    def y_half(p, way):
        slot = way % NY
        i = WAYS.index(way)
        cols = pl.ds(0, half) if way == 1 else pl.ds(half, half)
        return remote(
            main.at[p, slot, :, cols], main.at[p, NY // 2, :, cols], yh_s.at[p, i], yh_r.at[p, i], at(way, 0)
        )

    def y_rest(j):
        return remote(rest.at[0, 0], rest.at[0, j], r0_s.at[j], r0_r.at[j], at(j, 0))

    def stat_copy(p):
        return remote(stat_out.at[p], stat_in.at[p], st_s.at[p], st_r.at[p], at(0, -p))

    def sum_copy(j):
        return remote(sum_out, sum_in.at[j], s2_s.at[j], s2_r.at[j], at(-j, 0))

    def send_z(copy, parent):
        for k in SOURCE:
            if SOURCE[k] == parent:
                for way in WAYS:
                    copy(way, k).start()

    def planes(k):
        return (k,) if k in (0, LAST) else (plane(1, k), plane(-1, k))

    def on_main(k):
        for way in WAYS:
            z_main(way, k).wait_recv()
        send_z(z_main, k)
        fan_out(k)

    def fan_out(k):
        for p in planes(k):
            for way in WAYS:
                y_main(p, way).start()

    def on_rest(k):
        for way in WAYS:
            z_rest(way, k).wait_recv()
        send_z(z_rest, k)

    def on_y(k):
        for p in planes(k):
            for way in WAYS:
                y_main(p, way).wait_recv()
                y_half(p, way).start()

    def ready(*distances):
        for k in distances:
            for p in planes(k):
                for way in WAYS:
                    y_half(p, way).wait_recv()

    for fetch in fetches[:3]:
        fetch.wait()
    values = hid[...].astype(jnp.float32)
    square_mean = jnp.mean(values * values, axis=1, keepdims=True)
    normed = values * lax.rsqrt(square_mean + 1e-05) * gain[...][None, :]
    main[0, 0] = normed[0:MAIN].astype(jnp.bfloat16)
    rest[0, 0, :, 0:depth] = normed[MAIN:CAP].astype(jnp.bfloat16)
    place = lax.broadcasted_iota(jnp.int32, (REST, EXTRA), 1)
    wanted = jnp.zeros((REST, EXTRA), jnp.int32)
    for i in range(CAP):
        wanted = jnp.where(place == i, ids[i], wanted)
    first = lax.broadcasted_iota(jnp.int32, (REST, EXTRA), 0) == 0
    digits = jnp.where(first, wanted >> 8, wanted & 255)
    rest[0, 0, :, depth : depth + EXTRA] = digits.astype(jnp.float32).astype(jnp.bfloat16)
    turn[...] = jnp.zeros_like(turn)

    pl.semaphore_wait(barrier, len(near))
    for j in (2, 1, 3):
        y_rest(j).start()
    send_z(z_main, 0)
    fan_out(0)

    lane = lax.broadcasted_iota(jnp.int32, (8, 128), 1)
    sub = lax.broadcasted_iota(jnp.int32, (8, 128), 0)
    start_column = (me * vocab_dev).astype(jnp.float32)

    def fill(p, base):
        for j in range(NY):
            block[base + MAIN * j : base + MAIN * (j + 1), :] = main[p, j].astype(jnp.float32)
        for j in range(NY):
            rest32[REST * j : REST * (j + 1), :] = rest[p, j].astype(jnp.float32)
        block[base + MAIN * NY : base + ROWS, :] = rest32[:, 0:depth]
        digits8 = rest32[:, depth : depth + EXTRA]
        columns = []
        last = jnp.zeros((8, 128), jnp.float32)
        for j in range(NY):
            number = digits8[2 * j : 2 * j + 1] * 256.0 + digits8[2 * j + 1 : 2 * j + 2]
            number = jnp.broadcast_to(number, (8, 128))
            columns.append(jnp.sum(jnp.where(lane == sub, number, 0.0), axis=1, keepdims=True))
            last = jnp.where(sub // REST == j, number, last)
        columns.append(jnp.sum(jnp.where(lane == MAIN + lax.rem(sub, REST), last, 0.0), axis=1, keepdims=True))
        return columns

    def compute(members):
        columns = []
        for i, p in enumerate(members):
            columns += fill(p, ROWS * i)
        wanted_column = jnp.concatenate(columns, axis=0) - start_column
        lhs = block[...].astype(jnp.bfloat16)
        for n in range(0, vocab_dev, 256):
            logits[:, n : n + 256] = (
                jnp.dot(lhs, weight[:, n : n + 256], preferred_element_type=jnp.float32) * logit_scale
            )
        z = logits[...]
        peak = jnp.max(z, axis=1, keepdims=True)
        e = jnp.exp(z - peak)
        total = jnp.sum(e, axis=1, keepdims=True)
        moment = jnp.sum(e * z, axis=1, keepdims=True)
        column = lax.broadcasted_iota(jnp.int32, z.shape, 1).astype(jnp.float32)
        chosen = jnp.sum(jnp.where(column == wanted_column, z, 0.0), axis=1, keepdims=True)
        side = lax.broadcasted_iota(jnp.int32, (z.shape[0], 128), 1)
        stats = jnp.where(side == 0, peak, jnp.where(side == 1, total, jnp.where(side == 2, moment, chosen)))
        for i in range(len(members)):
            turn[64 * i : 64 * i + ROWS, :] = stats[ROWS * i : ROWS * (i + 1)]
        for i in range(0, len(members), 2):
            turned = jnp.transpose(turn[64 * i : 64 * i + 128, :])[0:8]
            stat_out[members[i]] = turned
            stat_out[members[i + 1]] = pltpu.roll(turned, 64, 1)

    on_main(1)
    for j in (1, 3, 2):
        y_rest(j).wait_recv()
    send_z(z_rest, 0)
    on_main(4)
    on_y(0)
    on_main(2)
    on_rest(1)
    on_y(1)
    on_main(6)
    on_main(5)
    on_rest(4)
    on_main(3)
    on_y(4)
    on_rest(2)
    on_y(2)
    on_main(7)
    on_main(8)
    on_rest(6)

    def group(b, carry):
        @pl.when(b == 0)
        def _():
            ready(1, 4)
            fetches[4].wait()

        @pl.when(b == 1)
        def _():
            on_y(5)
            on_y(6)
            on_y(3)
            on_y(7)
            on_y(8)
            on_rest(5)
            ready(2, 5)

        @pl.when(b == 2)
        def _():
            on_rest(3)
            ready(3, 6)

        @pl.when(b == 3)
        def _():
            on_rest(7)
            on_rest(8)
            ready(7, 8, 0)

        end = b == BLOCKS - 1
        low = jnp.where(end, 7, b + 1)
        high = jnp.where(end, LAST, b + 4)
        members = (low, NZ - low, high, jnp.where(end, 0, NZ - high))
        compute(members)
        for p in members[:3]:
            stat_copy(p).start()

        @pl.when(b < BLOCKS - 1)
        def _():
            stat_copy(members[3]).start()

        return carry

    lax.fori_loop(0, BLOCKS, group, 0)

    def merge(peaks, totals, moments, chosens):
        peak = jnp.max(peaks, axis=0, keepdims=True)
        factor = jnp.exp(peaks - peak)
        return (
            peak,
            jnp.sum(totals * factor, axis=0, keepdims=True),
            jnp.sum(moments * factor, axis=0, keepdims=True),
            jnp.sum(chosens, axis=0, keepdims=True),
        )

    stat_in[0] = stat_out[0]
    for p in range(1, NZ):
        stat_copy(p).wait_recv()
    peak, total, moment, chosen = merge(stat_in[:, 0], stat_in[:, 1], stat_in[:, 2], stat_in[:, 3])
    sums = jnp.where(sub == 0, peak, jnp.where(sub == 1, total, jnp.where(sub == 2, moment, chosen)))
    sum_out[...] = sums
    sum_in[0] = sums
    for j in (2, 1, 3):
        sum_copy(j).start()
    for j in (1, 3, 2):
        sum_copy(j).wait_recv()
    mine = []
    for j in range(NY):
        tile = sum_in[j]
        body = pltpu.roll(tile, (128 - MAIN * j) % 128, 1)
        tail = pltpu.roll(tile, (128 + MAIN - MAIN * NY - REST * j) % 128, 1)
        mine.append(jnp.where(lane < MAIN, body, tail))
    peak, total, moment, chosen = merge(
        *[jnp.concatenate([tile[i : i + 1] for tile in mine], axis=0) for i in range(4)]
    )
    log_total = jnp.log(total)
    fetches[3].wait()
    scored = lax.broadcasted_iota(jnp.int32, (1, 128), 1) < held[0]
    slots = out_ref.shape[1]
    out_ref[0:1, :] = jnp.where(scored, chosen - peak - log_total, 0.0)[:, 0:slots]
    out_ref[1:2, :] = jnp.where(scored, peak + log_total - moment / total, 0.0)[:, 0:slots]

    for j in range(1, NY):
        y_rest(j).wait_send()
        sum_copy(j).wait_send()
    for k in SOURCE:
        for way in WAYS:
            z_main(way, k).wait_send()
            z_rest(way, k).wait_send()
    for p in range(NZ):
        for way in WAYS:
            y_main(p, way).wait_send()
            y_half(p, way).wait_send()
        if p:
            stat_copy(p).wait_send()


def on_device(hidden, norm_gain, head_weight, targets, counts):
    slots, depth = hidden.shape
    vocab_dev = head_weight.shape[1]
    dma = pltpu.SemaphoreType.DMA
    any_spec = pl.BlockSpec(memory_space=pl.ANY)
    both = pl.pallas_call(
        kernel,
        out_shape=jax.ShapeDtypeStruct((2, slots), jnp.float32),
        in_specs=[any_spec] * 5,
        out_specs=pl.BlockSpec(memory_space=pltpu.VMEM),
        scratch_shapes=[
            pltpu.VMEM((slots, depth), jnp.bfloat16),
            pltpu.VMEM((depth,), jnp.float32),
            pltpu.VMEM((depth, vocab_dev), jnp.bfloat16),
            pltpu.SMEM((slots,), jnp.int32),
            pltpu.SMEM((1,), jnp.int32),
            pltpu.VMEM((NZ, NY, MAIN, depth), jnp.bfloat16),
            pltpu.VMEM((NZ, NY, REST, depth + EXTRA), jnp.bfloat16),
            pltpu.VMEM((NY * REST, depth + EXTRA), jnp.float32),
            pltpu.VMEM((BLOCKS * ROWS, depth), jnp.float32),
            pltpu.VMEM((BLOCKS * ROWS, vocab_dev), jnp.float32),
            pltpu.VMEM((256, 128), jnp.float32),
            pltpu.VMEM((NZ, 8, 128), jnp.float32),
            pltpu.VMEM((NZ, 8, 128), jnp.float32),
            pltpu.VMEM((8, 128), jnp.float32),
            pltpu.VMEM((NY, 8, 128), jnp.float32),
            dma((5,)),
            dma((NZ + 1,)), dma((NZ + 1,)),
            dma((NZ + 1,)), dma((NZ + 1,)),
            dma((NZ, 2)), dma((NZ, 2)),
            dma((NZ, 2)), dma((NZ, 2)),
            dma((NY,)), dma((NY,)),
            dma((NZ,)), dma((NZ,)),
            dma((NY,)), dma((NY,)),
        ],
        compiler_params=pltpu.CompilerParams(collective_id=0, has_side_effects=True),
    )(hidden, norm_gain, head_weight, targets, counts)
    return (both[0], both[1])


def solution(mesh):
    in_specs = (
        P(("req", "vocab"), None),
        P(),
        P(None, "vocab"),
        P(("req", "vocab")),
        P(("req", "vocab")),
    )
    out_specs = (P(("req", "vocab")), P(("req", "vocab")))
    return jax.shard_map(
        on_device, mesh=mesh, in_specs=in_specs, out_specs=out_specs, check_vma=False
    )
```

```python
import jax
import jax.numpy as jnp
from jax import lax
from jax.experimental import pallas as pl
from jax.experimental.pallas import tpu as pltpu
from jax.sharding import PartitionSpec as P

logit_scale = 256.0 / 2304.0
NY, NZ = 4, 16
CAP = 10
MAIN = 8
REST = CAP - MAIN
EXTRA = 128
ROWS = CAP * NY
LANES = 32
LAST = NZ // 2
SOURCE = {1: 0, 3: 0, 2: 1, 6: 3, 4: 3, 8: 6, 7: 6, 5: 6}
REST_FIRST = (3, 1, 2, 6, 4, 8, 7, 5)
DIRECT = ()
GROUPS = ((3, 13, 2, 14), (6, 10, 4, 12), (7, 9, 8, 11), (0, 1, 15, 5))
ORDER = (
    ("m1", "y0", "Y", "m3", "m2", "y1", "y3", "m6", "m4", "r3", "r1", "y2", "m7", "m5", "m8", "r2", "c2", "c3"),
    ("y6", "r6", "y4", "y7", "y8", "y5", "r4", "c6", "c4"),
    ("c7", "c8", "c5", "r5", "r7", "r8"),
    ("c0", "c1"),
)
WAYS = (1, -1)


def plane(way, k):
    return k * way % NZ


def kernel(
    hidden_hbm, gain_hbm, weight_hbm, targets_hbm, counts_hbm,
    out_ref,
    hid, gain, weight, ids, held, main, rest, rest32, block, logits, stat_out, stat_in,
    local_sem, zm_s, zm_r, zr_s, zr_r, ym_s, ym_r, yh_s, yh_r, r0_s, r0_r, st_s, st_r,
):
    depth = hid.shape[1]
    half = depth // 2
    vocab_dev = weight.shape[1]
    me = lax.axis_index("vocab")
    my_y, my_z = me // NZ, lax.rem(me, NZ)

    def at(dy, dz):
        return {"vocab": lax.rem(my_y + dy + NY, NY) * NZ + lax.rem(my_z + dz + NZ, NZ)}

    reach = sorted({abs(k - SOURCE[k]) for k in SOURCE})
    near = [at(0, way * k) for k in reach for way in WAYS] + [at(dy, 0) for dy in range(1, NY)]
    barrier = pltpu.get_barrier_semaphore()
    for device in near:
        pl.semaphore_signal(barrier, inc=1, device_id=device, device_id_type=pl.DeviceIdType.MESH)
    fetches = [
        pltpu.make_async_copy(src, dst, local_sem.at[i])
        for i, (src, dst) in enumerate(
            [(hidden_hbm, hid), (gain_hbm, gain), (targets_hbm, ids), (counts_hbm, held), (weight_hbm, weight)]
        )
    ]
    for fetch in fetches:
        fetch.start()

    def remote(src, dst, send, recv, device):
        return pltpu.make_async_remote_copy(
            src_ref=src, dst_ref=dst, send_sem=send, recv_sem=recv,
            device_id=device, device_id_type=pl.DeviceIdType.MESH,
        )

    def z_main(way, k):
        src, dst = plane(way, SOURCE[k]), plane(way, k)
        device = at(0, way * (k - SOURCE[k]))
        if k < LAST:
            return remote(main.at[src, 0], main.at[dst, 0], zm_s, zm_r.at[k], device)
        cols = pl.ds(0, half) if way == 1 else pl.ds(half, half)
        return remote(main.at[src, 0, :, cols], main.at[dst, 0, :, cols], zm_s, zm_r.at[k], device)

    def z_rest(way, k):
        src, dst = plane(way, SOURCE[k]), plane(way, k)
        device = at(0, way * (k - SOURCE[k]))
        if k < LAST:
            return remote(rest.at[src], rest.at[dst], zr_s, zr_r.at[k], device)
        part = pl.ds(0, NY // 2) if way == 1 else pl.ds(NY // 2, NY // 2)
        return remote(rest.at[src, part], rest.at[dst, part], zr_s, zr_r.at[k], device)

    def y_main(p, way):
        return remote(main.at[p, 0], main.at[p, way % NY], ym_s, ym_r.at[distance(p)], at(way, 0))

    def y_far(p):
        return remote(main.at[p, 0], main.at[p, NY // 2], ym_s, ym_r.at[distance(p)], at(NY // 2, 0))

    def y_half(p, way):
        cols = pl.ds(0, half) if way == 1 else pl.ds(half, half)
        return remote(
            main.at[p, way % NY, :, cols], main.at[p, NY // 2, :, cols], yh_s, yh_r.at[distance(p)], at(way, 0)
        )

    def y_rest(j):
        return remote(rest.at[0, 0], rest.at[0, j], r0_s, r0_r, at(j, 0))

    def stat_copy(p, j):
        return remote(stat_out.at[p, j], stat_in.at[p * NY + j], st_s, st_r, at(-j, -p))

    def arrive(view, sem):
        remote(view, view, local_sem.at[0], sem, at(1, 0)).wait_recv()

    def left(view, sem):
        remote(view, view, sem, local_sem.at[0], at(1, 0)).wait_send()

    def distance(p):
        return min(p, NZ - p)

    def planes(k):
        return (k,) if k in (0, LAST) else (plane(1, k), plane(-1, k))

    def send_z(copy, parent):
        for k in REST_FIRST if copy is z_rest else SOURCE:
            if SOURCE[k] == parent:
                for way in WAYS:
                    copy(way, k).start()

    def fan_out(k):
        for p in planes(k):
            if k in DIRECT:
                y_far(p).start()
            for way in WAYS:
                y_main(p, way).start()

    def on_main(k):
        arrive(main.at[pl.ds(0, len(planes(k))), 0], zm_r.at[k])
        send_z(z_main, k)
        fan_out(k)

    def on_rest(k):
        arrive(rest.at[pl.ds(0, len(planes(k)))], zr_r.at[k])
        send_z(z_rest, k)

    def on_own_rest():
        arrive(rest.at[0, pl.ds(1, NY - 1)], r0_r)
        send_z(z_rest, 0)

    def on_y(k):
        arrive(main.at[0, pl.ds(0, 2 * len(planes(k)))], ym_r.at[k])
        for p in planes(k):
            for way in WAYS:
                y_half(p, way).start()

    def complete(k):
        if k in DIRECT:
            arrive(main.at[pl.ds(0, len(planes(k))), pl.ds(0, NY - 1)], ym_r.at[k])
        else:
            arrive(main.at[pl.ds(0, len(planes(k))), NY // 2], yh_r.at[k])

    def follow(order):
        for word in order:
            if word == "Y":
                on_own_rest()
            else:
                {"m": on_main, "r": on_rest, "y": on_y, "c": complete}[word[0]](int(word[1:]))

    for fetch in fetches[:3]:
        fetch.wait()
    values = hid[...].astype(jnp.float32)
    square_mean = jnp.mean(values * values, axis=1, keepdims=True)
    normed = values * lax.rsqrt(square_mean + 1e-05) * gain[...][None, :]
    main[0, 0] = normed[0:MAIN].astype(jnp.bfloat16)
    rest[0, 0, :, 0:depth] = normed[MAIN:CAP].astype(jnp.bfloat16)
    place = lax.broadcasted_iota(jnp.int32, (REST, EXTRA), 1)
    wanted = jnp.zeros((REST, EXTRA), jnp.int32)
    for i in range(CAP):
        wanted = jnp.where(place == i, ids[i], wanted)
    first = lax.broadcasted_iota(jnp.int32, (REST, EXTRA), 0) == 0
    digits = jnp.where(first, wanted >> 8, wanted & 255)
    rest[0, 0, :, depth : depth + EXTRA] = digits.astype(jnp.float32).astype(jnp.bfloat16)

    pl.semaphore_wait(barrier, len(near))
    for j in (2, 1, 3):
        y_rest(j).start()
    send_z(z_main, 0)
    fan_out(0)

    lane = lax.broadcasted_iota(jnp.int32, (8, 128), 1)
    sub = lax.broadcasted_iota(jnp.int32, (8, 128), 0)
    start_column = (me * vocab_dev).astype(jnp.float32)

    def fill(p, base):
        for j in range(NY):
            block[base + MAIN * j : base + MAIN * (j + 1), :] = main[p, j].astype(jnp.float32)
        for j in range(NY):
            rest32[REST * j : REST * (j + 1), :] = rest[p, j].astype(jnp.float32)
        block[base + MAIN * NY : base + ROWS, :] = rest32[:, 0:depth]
        digits8 = rest32[:, depth : depth + EXTRA]
        columns = []
        last = jnp.zeros((8, 128), jnp.float32)
        for j in range(NY):
            number = digits8[2 * j : 2 * j + 1] * 256.0 + digits8[2 * j + 1 : 2 * j + 2]
            number = jnp.broadcast_to(number, (8, 128))
            columns.append(jnp.sum(jnp.where(lane == sub, number, 0.0), axis=1, keepdims=True))
            last = jnp.where(sub // REST == j, number, last)
        columns.append(jnp.sum(jnp.where(lane == MAIN + lax.rem(sub, REST), last, 0.0), axis=1, keepdims=True))
        return columns

    def compute(members):
        columns = []
        for i, p in enumerate(members):
            columns += fill(p, ROWS * i)
        wanted_column = jnp.concatenate(columns, axis=0) - start_column
        lhs = block[...].astype(jnp.bfloat16)
        for n in range(0, vocab_dev, 256):
            logits[:, n : n + 256] = (
                jnp.dot(lhs, weight[:, n : n + 256], preferred_element_type=jnp.float32) * logit_scale
            )
        z = logits[...]
        peak = jnp.max(z, axis=1, keepdims=True)
        e = jnp.exp(z - peak)
        total = jnp.sum(e, axis=1, keepdims=True)
        moment = jnp.sum(e * z, axis=1, keepdims=True)
        column = lax.broadcasted_iota(jnp.int32, z.shape, 1).astype(jnp.float32)
        chosen = jnp.sum(jnp.where(column == wanted_column, z, 0.0), axis=1, keepdims=True)
        stats = (peak, total, moment, chosen)
        for i, p in enumerate(members):
            chunks = [[stat[ROWS * i + 8 * c : ROWS * i + 8 * (c + 1)] for stat in stats] for c in range(NY + 1)]
            last = jnp.zeros((8, 128), jnp.float32)
            for n, stat in enumerate(chunks[NY]):
                last = jnp.where(lane == LANES * n + MAIN + lax.rem(sub, REST), stat, last)
            for j in range(NY):
                tile = jnp.where(sub // REST == j, last, 0.0)
                for n, stat in enumerate(chunks[j]):
                    tile = jnp.where(lane == LANES * n + sub, stat, tile)
                stat_out[p, j] = jnp.sum(tile, axis=0, keepdims=True)

    def group(b, carry):
        for i, members in enumerate(GROUPS):

            @pl.when(b == i)
            def _():
                follow(ORDER[i])
                if i == 0:
                    fetches[4].wait()

        members = []
        for i in range(len(GROUPS[0])):
            p = jnp.int32(GROUPS[0][i])
            for j in range(1, len(GROUPS)):
                p = jnp.where(b == j, GROUPS[j][i], p)
            members.append(p)
        compute(members)
        for i, p in enumerate(members):
            for j in range(NY):
                if (i, j) != (0, 0):
                    stat_copy(p, j).start()

        @pl.when(b < len(GROUPS) - 1)
        def _():
            stat_copy(members[0], 0).start()

        return carry

    lax.fori_loop(0, len(GROUPS), group, 0)

    left(rest.at[0, pl.ds(1, NY - 1)], r0_s)
    left(main.at[pl.ds(0, NZ - 1), 0], zm_s)
    left(rest.at[pl.ds(0, NZ - 1)], zr_s)
    far = sum(len(planes(k)) for k in DIRECT)
    left(main.at[pl.ds(0, NZ), pl.ds(0, 2)], ym_s)
    if far:
        left(main.at[pl.ds(0, far), 0], ym_s)
    left(main.at[pl.ds(0, NZ - far), 0], yh_s)

    stat_in[0] = stat_out[0, 0]
    arrive(stat_in.at[pl.ds(1, NY * NZ - 1)], st_r)
    parts = stat_in[...].reshape(NY * NZ, 128)
    peak = jnp.max(parts, axis=0, keepdims=True)
    factor = jnp.exp(parts - peak)
    spot = lax.broadcasted_iota(jnp.int32, parts.shape, 1) // LANES
    factor = jnp.where(
        spot == 1,
        pltpu.roll(factor, LANES, 1),
        jnp.where(spot == 2, pltpu.roll(factor, 2 * LANES, 1), 1.0),
    )
    sums = jnp.broadcast_to(jnp.sum(parts * factor, axis=0, keepdims=True), (8, 128))
    total, moment, chosen = [pltpu.roll(sums, 128 - LANES * n, 1)[0:1] for n in (1, 2, 3)]
    log_total = jnp.log(total)
    fetches[3].wait()
    scored = lax.broadcasted_iota(jnp.int32, (1, 128), 1) < held[0]
    slots = out_ref.shape[1]
    out_ref[0:1, :] = jnp.where(scored, chosen - peak - log_total, 0.0)[:, 0:slots]
    out_ref[1:2, :] = jnp.where(scored, peak + log_total - moment / total, 0.0)[:, 0:slots]
    left(stat_in.at[pl.ds(1, NY * NZ - 1)], st_s)


def on_device(hidden, norm_gain, head_weight, targets, counts):
    slots, depth = hidden.shape
    vocab_dev = head_weight.shape[1]
    dma = pltpu.SemaphoreType.DMA
    any_spec = pl.BlockSpec(memory_space=pl.ANY)
    both = pl.pallas_call(
        kernel,
        out_shape=jax.ShapeDtypeStruct((2, slots), jnp.float32),
        in_specs=[any_spec] * 5,
        out_specs=pl.BlockSpec(memory_space=pltpu.VMEM),
        scratch_shapes=[
            pltpu.VMEM((slots, depth), jnp.bfloat16),
            pltpu.VMEM((depth,), jnp.float32),
            pltpu.VMEM((depth, vocab_dev), jnp.bfloat16),
            pltpu.SMEM((slots,), jnp.int32),
            pltpu.SMEM((1,), jnp.int32),
            pltpu.VMEM((NZ, NY, MAIN, depth), jnp.bfloat16),
            pltpu.VMEM((NZ, NY, REST, depth + EXTRA), jnp.bfloat16),
            pltpu.VMEM((NY * REST, depth + EXTRA), jnp.float32),
            pltpu.VMEM((4 * ROWS, depth), jnp.float32),
            pltpu.VMEM((4 * ROWS, vocab_dev), jnp.float32),
            pltpu.VMEM((NZ, NY, 1, 128), jnp.float32),
            pltpu.VMEM((NZ * NY, 1, 128), jnp.float32),
            dma((5,)),
            dma, dma((LAST + 1,)),
            dma, dma((LAST + 1,)),
            dma, dma((LAST + 1,)),
            dma, dma((LAST + 1,)),
            dma, dma,
            dma, dma,
        ],
        compiler_params=pltpu.CompilerParams(collective_id=0, has_side_effects=True),
    )(hidden, norm_gain, head_weight, targets, counts)
    return (both[0], both[1])


def solution(mesh):
    in_specs = (
        P(("req", "vocab"), None),
        P(),
        P(None, "vocab"),
        P(("req", "vocab")),
        P(("req", "vocab")),
    )
    out_specs = (P(("req", "vocab")), P(("req", "vocab")))
    return jax.shard_map(
        on_device, mesh=mesh, in_specs=in_specs, out_specs=out_specs, check_vma=False
    )
```

```python
import jax
import jax.numpy as jnp
from jax import lax
from jax.experimental import pallas as pl
from jax.experimental.pallas import tpu as pltpu
from jax.sharding import PartitionSpec as P

logit_scale = 256.0 / 2304.0
NY, NZ = 4, 16
CAP = 10
MAIN = 8
REST = CAP - MAIN
EXTRA = 128
ROWS = CAP * NY
LANES = 32
LAST = NZ // 2
SOURCE = {2: 0, 1: 0, 4: 2, 3: 2, 6: 4, 5: 4, 8: 6, 7: 6}
DIRECT = (7, 8)
GROUPS = ((1, 15, 2, 14), (3, 13, 4, 12), (7, 9, 8, 6), (0, 5, 11, 10))
ORDER = (
    ("m2", "m1", "y0", "Y", "m4", "s1", "y1", "m3", "y2", "r2", "m6", "s3", "m5", "y4", "y3", "r4", "m8", "m7", "y6", "s5", "r1", "c1", "c2"),
    ("r6", "s7", "y5", "r3", "c4", "c3"),
    ("c7", "c8", "c6", "r7", "r8"),
    ("c0", "c5", "r5"),
)
WAYS = (1, -1)


def plane(way, k):
    return k * way % NZ


def kernel(
    hidden_hbm, gain_hbm, weight_hbm, targets_hbm, counts_hbm,
    out_ref,
    hid, gain, weight, ids, held, main, rest, rest32, block, logits, stat_out, stat_in,
    local_sem, zm_s, zm_r, zr_s, zr_r, ym_s, ym_r, yh_s, yh_r, r0_s, r0_r, st_s, st_r,
):
    depth = hid.shape[1]
    half = depth // 2
    vocab_dev = weight.shape[1]
    me = lax.axis_index("vocab")
    my_y, my_z = me // NZ, lax.rem(me, NZ)

    def at(dy, dz):
        return {"vocab": lax.rem(my_y + dy + NY, NY) * NZ + lax.rem(my_z + dz + NZ, NZ)}

    reach = sorted({abs(k - SOURCE[k]) for k in SOURCE})
    near = [at(0, way * k) for k in reach for way in WAYS] + [at(dy, 0) for dy in range(1, NY)]
    barrier = pltpu.get_barrier_semaphore()
    for device in near:
        pl.semaphore_signal(barrier, inc=1, device_id=device, device_id_type=pl.DeviceIdType.MESH)
    fetches = [
        pltpu.make_async_copy(src, dst, local_sem.at[i])
        for i, (src, dst) in enumerate(
            [(hidden_hbm, hid), (gain_hbm, gain), (targets_hbm, ids), (counts_hbm, held), (weight_hbm, weight)]
        )
    ]
    for fetch in fetches:
        fetch.start()

    def remote(src, dst, send, recv, device):
        return pltpu.make_async_remote_copy(
            src_ref=src, dst_ref=dst, send_sem=send, recv_sem=recv,
            device_id=device, device_id_type=pl.DeviceIdType.MESH,
        )

    def z_main(way, k):
        src, dst = plane(way, SOURCE[k]), plane(way, k)
        device = at(0, way * (k - SOURCE[k]))
        if k < LAST:
            return remote(main.at[src, 0], main.at[dst, 0], zm_s, zm_r.at[k], device)
        cols = pl.ds(0, half) if way == 1 else pl.ds(half, half)
        return remote(main.at[src, 0, :, cols], main.at[dst, 0, :, cols], zm_s, zm_r.at[k], device)

    def z_rest(way, k):
        src, dst = plane(way, SOURCE[k]), plane(way, k)
        device = at(0, way * (k - SOURCE[k]))
        if k < LAST:
            return remote(rest.at[src], rest.at[dst], zr_s, zr_r.at[k], device)
        part = pl.ds(0, NY // 2) if way == 1 else pl.ds(NY // 2, NY // 2)
        return remote(rest.at[src, part], rest.at[dst, part], zr_s, zr_r.at[k], device)

    def y_main(p, way):
        return remote(main.at[p, 0], main.at[p, way % NY], ym_s, ym_r.at[distance(p)], at(way, 0))

    def y_far(p):
        return remote(main.at[p, 0], main.at[p, NY // 2], ym_s, ym_r.at[distance(p)], at(NY // 2, 0))

    def y_half(p, way):
        cols = pl.ds(0, half) if way == 1 else pl.ds(half, half)
        return remote(
            main.at[p, way % NY, :, cols], main.at[p, NY // 2, :, cols], yh_s, yh_r.at[distance(p)], at(way, 0)
        )

    def y_rest(j):
        return remote(rest.at[0, 0], rest.at[0, j], r0_s, r0_r, at(j, 0))

    def stat_copy(p, j):
        return remote(stat_out.at[p, j], stat_in.at[p * NY + j], st_s, st_r, at(-j, -p))

    def arrive(view, sem):
        remote(view, view, local_sem.at[0], sem, at(1, 0)).wait_recv()

    def left(view, sem):
        remote(view, view, sem, local_sem.at[0], at(1, 0)).wait_send()

    def distance(p):
        return min(p, NZ - p)

    def planes(k):
        return (k,) if k in (0, LAST) else (plane(1, k), plane(-1, k))

    def send_z(copy, parent, odd=True):
        for k in SOURCE:
            if SOURCE[k] == parent and (odd or k % 2 == 0):
                for way in WAYS:
                    copy(way, k).start()

    def send_rest(k):
        for way in WAYS:
            z_rest(way, k).start()

    def fan_out(k):
        for p in planes(k):
            if k in DIRECT:
                y_far(p).start()
            for way in WAYS:
                y_main(p, way).start()

    def on_main(k):
        arrive(main.at[pl.ds(0, len(planes(k))), 0], zm_r.at[k])
        send_z(z_main, k)
        fan_out(k)

    def on_rest(k):
        arrive(rest.at[pl.ds(0, len(planes(k)))], zr_r.at[k])
        send_z(z_rest, k, odd=False)

    def on_own_rest():
        arrive(rest.at[0, pl.ds(1, NY - 1)], r0_r)
        send_z(z_rest, 0, odd=False)

    def on_y(k):
        arrive(main.at[0, pl.ds(0, 2 * len(planes(k)))], ym_r.at[k])
        for p in planes(k):
            for way in WAYS:
                y_half(p, way).start()

    def complete(k):
        if k in DIRECT:
            arrive(main.at[pl.ds(0, len(planes(k))), pl.ds(0, NY - 1)], ym_r.at[k])
        else:
            arrive(main.at[pl.ds(0, len(planes(k))), NY // 2], yh_r.at[k])

    def follow(order):
        for word in order:
            if word == "Y":
                on_own_rest()
            else:
                {"m": on_main, "r": on_rest, "s": send_rest, "y": on_y, "c": complete}[word[0]](int(word[1:]))

    for fetch in fetches[:3]:
        fetch.wait()
    values = hid[...].astype(jnp.float32)
    square_mean = jnp.mean(values * values, axis=1, keepdims=True)
    normed = values * lax.rsqrt(square_mean + 1e-05) * gain[...][None, :]
    main[0, 0] = normed[0:MAIN].astype(jnp.bfloat16)
    rest[0, 0, :, 0:depth] = normed[MAIN:CAP].astype(jnp.bfloat16)
    place = lax.broadcasted_iota(jnp.int32, (REST, EXTRA), 1)
    wanted = jnp.zeros((REST, EXTRA), jnp.int32)
    for i in range(CAP):
        wanted = jnp.where(place == i, ids[i], wanted)
    first = lax.broadcasted_iota(jnp.int32, (REST, EXTRA), 0) == 0
    digits = jnp.where(first, wanted >> 8, wanted & 255)
    rest[0, 0, :, depth : depth + EXTRA] = digits.astype(jnp.float32).astype(jnp.bfloat16)

    pl.semaphore_wait(barrier, len(near))
    for j in (2, 1, 3):
        y_rest(j).start()
    send_z(z_main, 0)
    fan_out(0)

    lane = lax.broadcasted_iota(jnp.int32, (8, 128), 1)
    sub = lax.broadcasted_iota(jnp.int32, (8, 128), 0)
    start_column = (me * vocab_dev).astype(jnp.float32)

    def fill(p, base):
        for j in range(NY):
            block[base + MAIN * j : base + MAIN * (j + 1), :] = main[p, j].astype(jnp.float32)
        for j in range(NY):
            rest32[REST * j : REST * (j + 1), :] = rest[p, j].astype(jnp.float32)
        block[base + MAIN * NY : base + ROWS, :] = rest32[:, 0:depth]
        digits8 = rest32[:, depth : depth + EXTRA]
        columns = []
        last = jnp.zeros((8, 128), jnp.float32)
        for j in range(NY):
            number = digits8[2 * j : 2 * j + 1] * 256.0 + digits8[2 * j + 1 : 2 * j + 2]
            number = jnp.broadcast_to(number, (8, 128))
            columns.append(jnp.sum(jnp.where(lane == sub, number, 0.0), axis=1, keepdims=True))
            last = jnp.where(sub // REST == j, number, last)
        columns.append(jnp.sum(jnp.where(lane == MAIN + lax.rem(sub, REST), last, 0.0), axis=1, keepdims=True))
        return columns

    def compute(members):
        columns = []
        for i, p in enumerate(members):
            columns += fill(p, ROWS * i)
        wanted_column = jnp.concatenate(columns, axis=0) - start_column
        lhs = block[...].astype(jnp.bfloat16)
        for n in range(0, vocab_dev, 256):
            logits[:, n : n + 256] = (
                jnp.dot(lhs, weight[:, n : n + 256], preferred_element_type=jnp.float32) * logit_scale
            )
        z = logits[...]
        peak = jnp.max(z, axis=1, keepdims=True)
        e = jnp.exp(z - peak)
        total = jnp.sum(e, axis=1, keepdims=True)
        moment = jnp.sum(e * z, axis=1, keepdims=True)
        column = lax.broadcasted_iota(jnp.int32, z.shape, 1).astype(jnp.float32)
        chosen = jnp.sum(jnp.where(column == wanted_column, z, 0.0), axis=1, keepdims=True)
        stats = (peak, total, moment, chosen)
        for i, p in enumerate(members):
            chunks = [[stat[ROWS * i + 8 * c : ROWS * i + 8 * (c + 1)] for stat in stats] for c in range(NY + 1)]
            last = jnp.zeros((8, 128), jnp.float32)
            for n, stat in enumerate(chunks[NY]):
                last = jnp.where(lane == LANES * n + MAIN + lax.rem(sub, REST), stat, last)
            for j in range(NY):
                tile = jnp.where(sub // REST == j, last, 0.0)
                for n, stat in enumerate(chunks[j]):
                    tile = jnp.where(lane == LANES * n + sub, stat, tile)
                stat_out[p, j] = jnp.sum(tile, axis=0, keepdims=True)

    def group(b, carry):
        for i, members in enumerate(GROUPS):

            @pl.when(b == i)
            def _():
                follow(ORDER[i])
                if i == 0:
                    fetches[4].wait()

        members = []
        for i in range(len(GROUPS[0])):
            p = jnp.int32(GROUPS[0][i])
            for j in range(1, len(GROUPS)):
                p = jnp.where(b == j, GROUPS[j][i], p)
            members.append(p)
        compute(members)
        for i, p in enumerate(members):
            for j in range(NY):
                if (i, j) != (0, 0):
                    stat_copy(p, j).start()

        @pl.when(b < len(GROUPS) - 1)
        def _():
            stat_copy(members[0], 0).start()

        return carry

    lax.fori_loop(0, len(GROUPS), group, 0)

    left(rest.at[0, pl.ds(1, NY - 1)], r0_s)
    left(main.at[pl.ds(0, NZ - 1), 0], zm_s)
    left(rest.at[pl.ds(0, NZ - 1)], zr_s)
    far = sum(len(planes(k)) for k in DIRECT)
    left(main.at[pl.ds(0, NZ), pl.ds(0, 2)], ym_s)
    if far:
        left(main.at[pl.ds(0, far), 0], ym_s)
    left(main.at[pl.ds(0, NZ - far), 0], yh_s)

    stat_in[0] = stat_out[0, 0]
    arrive(stat_in.at[pl.ds(1, NY * NZ - 1)], st_r)
    parts = stat_in[...].reshape(NY * NZ, 128)
    peak = jnp.max(parts, axis=0, keepdims=True)
    factor = jnp.exp(parts - peak)
    spot = lax.broadcasted_iota(jnp.int32, parts.shape, 1) // LANES
    factor = jnp.where(
        spot == 1,
        pltpu.roll(factor, LANES, 1),
        jnp.where(spot == 2, pltpu.roll(factor, 2 * LANES, 1), 1.0),
    )
    sums = jnp.broadcast_to(jnp.sum(parts * factor, axis=0, keepdims=True), (8, 128))
    total, moment, chosen = [pltpu.roll(sums, 128 - LANES * n, 1)[0:1] for n in (1, 2, 3)]
    log_total = jnp.log(total)
    fetches[3].wait()
    scored = lax.broadcasted_iota(jnp.int32, (1, 128), 1) < held[0]
    slots = out_ref.shape[1]
    out_ref[0:1, :] = jnp.where(scored, chosen - peak - log_total, 0.0)[:, 0:slots]
    out_ref[1:2, :] = jnp.where(scored, peak + log_total - moment / total, 0.0)[:, 0:slots]
    left(stat_in.at[pl.ds(1, NY * NZ - 1)], st_s)


def on_device(hidden, norm_gain, head_weight, targets, counts):
    slots, depth = hidden.shape
    vocab_dev = head_weight.shape[1]
    dma = pltpu.SemaphoreType.DMA
    any_spec = pl.BlockSpec(memory_space=pl.ANY)
    both = pl.pallas_call(
        kernel,
        out_shape=jax.ShapeDtypeStruct((2, slots), jnp.float32),
        in_specs=[any_spec] * 5,
        out_specs=pl.BlockSpec(memory_space=pltpu.VMEM),
        scratch_shapes=[
            pltpu.VMEM((slots, depth), jnp.bfloat16),
            pltpu.VMEM((depth,), jnp.float32),
            pltpu.VMEM((depth, vocab_dev), jnp.bfloat16),
            pltpu.SMEM((slots,), jnp.int32),
            pltpu.SMEM((1,), jnp.int32),
            pltpu.VMEM((NZ, NY, MAIN, depth), jnp.bfloat16),
            pltpu.VMEM((NZ, NY, REST, depth + EXTRA), jnp.bfloat16),
            pltpu.VMEM((NY * REST, depth + EXTRA), jnp.float32),
            pltpu.VMEM((4 * ROWS, depth), jnp.float32),
            pltpu.VMEM((4 * ROWS, vocab_dev), jnp.float32),
            pltpu.VMEM((NZ, NY, 1, 128), jnp.float32),
            pltpu.VMEM((NZ * NY, 1, 128), jnp.float32),
            dma((5,)),
            dma, dma((LAST + 1,)),
            dma, dma((LAST + 1,)),
            dma, dma((LAST + 1,)),
            dma, dma((LAST + 1,)),
            dma, dma,
            dma, dma,
        ],
        compiler_params=pltpu.CompilerParams(collective_id=0, has_side_effects=True),
    )(hidden, norm_gain, head_weight, targets, counts)
    return (both[0], both[1])


def solution(mesh):
    in_specs = (
        P(("req", "vocab"), None),
        P(),
        P(None, "vocab"),
        P(("req", "vocab")),
        P(("req", "vocab")),
    )
    out_specs = (P(("req", "vocab")), P(("req", "vocab")))
    return jax.shard_map(
        on_device, mesh=mesh, in_specs=in_specs, out_specs=out_specs, check_vma=False
    )
```
